128 devices in a mesh: tier: 8 (over y, z_lo), tile: 16 (over x, z_hi, core).
Axes of the slice: x: 4, y: 4, z: 4 (z_hi: 2, z_lo: 2; z = z_hi * 2 + z_lo), core: 2. Of those that a mesh axis runs over, the one named last changes fastest.
Arguments:
- warming_above_ambient: float32 [8, 16, 512, 2048], P('tier', None, 'tile'), may hold values from -6 to 6
- substance_label: int32 [8, 16, 512, 2048], P('tier', None, 'tile'), may hold values from 0 to 15
- glue_zone_label: int32 [512, 2048], P('tile'), may hold values from 0 to 7
- patch_label_per_cell: int32 [8, 512, 2048], P('tier', 'tile'), may hold values from 0 to 127
- heat_conductance_per_substance: float32 [16], replicated, may hold values from 0.3 to 4
- dissipation_per_patch: float32 [8, 128], P('tier'), may hold values from 0.5 to 5
- glue_sheet_reciprocal_operators: float32 [8, 16, 16], replicated, may hold values from -0.3 to 1.3, as said below
Outputs:
- final_state: float32 [8, 16, 512, 2048], P('tier', None, 'tile')
The draws below stay inside these ranges and needn't reach their ends.
Inputs may be any that keep to these rules, and one draw needn't show every extreme that they name: `glue_sheet_reciprocal_operators`: each matrix has diagonal entries of 0.6 to 1.0 plus a perturbation, and perturbed entries elsewhere.
All inputs are finite; a program needn't handle non-finite values.
Results may differ from the reference program's by a relative error of at most 0.0001.
Values sent between devices are 32-bit elements; how exact they have to be, the bound alone decides.
A program may use at most 128 MiB of HBM per device.

```python
import math
import jax
import jax.numpy as jnp
from jax import lax

DIE_NUMBER = 8
BLOCK = 16
SHEETS_PER_DIE = 16
GRID_WIDTH_CELLS = 2048
GRID_DEPTH_CELLS = 512
MATERIALS = 16
REGIONS = 8
POWER_TILES = 128
STEPS = 2


def draw_glue_sheet_reciprocal_operators(key, part):
    first, second = jax.random.split(key)
    diag = jax.random.uniform(first, (REGIONS, BLOCK), jnp.float32, 0.6, 1.0)
    other = jnp.clip(0.1 * jax.random.normal(second, (REGIONS, BLOCK, BLOCK), jnp.float32), -0.3, 0.3)
    eye = jnp.eye(BLOCK, dtype=jnp.float32)
    return eye * diag[:, :, None] + other


def place_ends(result, key, least, high):
    extent = result.shape
    index_at = [jax.random.randint(jax.random.fold_in(key, axis), (), 0, extent[axis]) for axis in range(len(extent))]
    result = result.at[tuple(index_at)].set(least)
    longest = extent.index(max(extent))
    index_at[longest] = (index_at[longest] + 1) % extent[longest]
    return result.at[tuple(index_at)].set(high)


def level_of(own_key, extent, pieces, least, largest):
    loudness = 1.0
    for position, blocks in pieces:
        steps = jax.random.uniform(jax.random.fold_in(jax.random.fold_in(own_key, 6), position), (blocks,), jnp.float32, least / len(pieces), largest / len(pieces))
        loudness = loudness * jnp.repeat(jnp.exp(steps), extent[position] // blocks).reshape((-1,) + (1,) * (len(extent) - 1 - position))
    return loudness


def normal_values(key, extent, spread, most, pieces=(), kind=jnp.bfloat16):
    loudness = level_of(key, extent, pieces, -0.22, 0.18) if pieces else 1.0
    drawn = jax.random.normal(key, extent, jnp.float32) * spread * loudness
    return jnp.minimum(jnp.maximum(drawn, -most), most).astype(kind)


def setup_inputs(seed: int = 0) -> dict:
    key_list = jax.random.split(jax.random.key(seed), 8)
    return {
        "warming_above_ambient": normal_values(key_list[0], (DIE_NUMBER, SHEETS_PER_DIE, GRID_DEPTH_CELLS, GRID_WIDTH_CELLS), 1.0, 6.0, ((0, 8), (2, 16)), jnp.float32),
        "substance_label": place_ends(jax.random.randint(key_list[1], (DIE_NUMBER, SHEETS_PER_DIE, GRID_DEPTH_CELLS, GRID_WIDTH_CELLS), 0, MATERIALS), jax.random.fold_in(key_list[1], 1), 0, MATERIALS - 1).astype(jnp.int32),
        "glue_zone_label": place_ends(jax.random.randint(key_list[2], (GRID_DEPTH_CELLS, GRID_WIDTH_CELLS), 0, REGIONS), jax.random.fold_in(key_list[2], 1), 0, REGIONS - 1).astype(jnp.int32),
        "patch_label_per_cell": place_ends(jax.random.randint(key_list[3], (DIE_NUMBER, GRID_DEPTH_CELLS, GRID_WIDTH_CELLS), 0, POWER_TILES), jax.random.fold_in(key_list[3], 1), 0, POWER_TILES - 1).astype(jnp.int32),
        "heat_conductance_per_substance": jnp.clip(jnp.exp(jax.random.uniform(key_list[4], (MATERIALS,), jnp.float32, math.log(0.3), math.log(4.0))), 0.3, 4.0),
        "dissipation_per_patch": jnp.clip(jnp.exp(math.log(5.0) - 2.3025851 * jax.random.uniform(key_list[5], (DIE_NUMBER, POWER_TILES), jnp.float32) ** level_of(key_list[5], (DIE_NUMBER, POWER_TILES), ((0, 8),), -0.2, 0.2)), 0.5, 5.0),
        "glue_sheet_reciprocal_operators": draw_glue_sheet_reciprocal_operators(jax.random.fold_in(key_list[7], 71), 0),
    }


step_dt = 0.04


def pad_axis(field, axis, low, high):
    widths = [(0, 0)] * field.ndim
    widths[axis] = (low, high)
    return jnp.pad(field, widths)


def conduct(padded_t, padded_k):
    centre = padded_t[..., 1:-1, :]
    kcell = padded_k[..., 1:-1, :]
    flux = 0.5 * (kcell + padded_k[..., 2:, :]) * (padded_t[..., 2:, :] - centre)
    flux = flux + 0.5 * (kcell + padded_k[..., :-2, :]) * (padded_t[..., :-2, :] - centre)
    side_t = pad_axis(centre, centre.ndim - 1, 1, 1)
    side_k = pad_axis(kcell, kcell.ndim - 1, 1, 1)
    flux = flux + 0.5 * (kcell + side_k[..., 2:]) * (side_t[..., 2:] - centre)
    flux = flux + 0.5 * (kcell + side_k[..., :-2]) * (side_t[..., :-2] - centre)
    face = 0.5 * (kcell[..., 1:, :, :] + kcell[..., :-1, :, :]) * (centre[..., 1:, :, :] - centre[..., :-1, :, :])
    axis = centre.ndim - 3
    return flux + pad_axis(face, axis, 0, 1) - pad_axis(face, axis, 1, 0)


def reference(warming_above_ambient, substance_label, glue_zone_label, patch_label_per_cell, heat_conductance_per_substance, dissipation_per_patch, glue_sheet_reciprocal_operators):
    kappa = heat_conductance_per_substance[substance_label]
    source = dissipation_per_patch[jnp.arange(DIE_NUMBER)[:, None, None], patch_label_per_cell]
    heating_snapshot = warming_above_ambient
    for step in range(STEPS):
        padded_t = pad_axis(heating_snapshot, 2, 1, 1)
        padded_k = pad_axis(kappa, 2, 1, 1)
        heating_snapshot = heating_snapshot + step_dt * conduct(padded_t, padded_k)
        heating_snapshot = heating_snapshot.at[:, 0].add(step_dt * source)
        planes = jnp.stack([heating_snapshot[:, 0], heating_snapshot[:, -1]], 1).reshape(2 * DIE_NUMBER, GRID_DEPTH_CELLS, GRID_WIDTH_CELLS)
        solved = jnp.zeros_like(planes)
        for which in range(REGIONS):
            mapped = jnp.einsum("ij,jxc->ixc", glue_sheet_reciprocal_operators[which], planes, precision=lax.Precision.HIGHEST)
            solved = solved + jnp.where(glue_zone_label == which, mapped, 0.0)
        solved = solved.reshape(DIE_NUMBER, 2, GRID_DEPTH_CELLS, GRID_WIDTH_CELLS)
        heating_snapshot = heating_snapshot.at[:, 0].set(solved[:, 0]).at[:, -1].set(solved[:, 1])
    return heating_snapshot
```

```python
import functools

import jax
import jax.numpy as jnp
from jax import lax
from jax.experimental import pallas as pl
from jax.experimental.pallas import tpu as pltpu
from jax.sharding import PartitionSpec as P

STEPS = 2
STEP_DT = 0.04
MESH = pl.DeviceIdType.MESH
F32 = jnp.float32


def lookup(table, index):
    return jnp.take_along_axis(table, index, axis=1, mode="promise_in_bounds")


def heat_kernel(
    dims,
    t_hbm, lab_hbm, zone_hbm, patch_hbm, ktab, stab, mtab,
    out_hbm,
    t0, lab, t1, kk, t2, zone, patch, src, coef, planes, rx, part, solved, back,
    hs, hr, ks, kr,
    load_sem, out_sem, hs_sem, hr_sem, ks_sem, kr_sem,
    fs_sem, fr_sem, bs_sem, br_sem, own_sem,
):
    nt, nk, nl, nc, regions = dims
    per = nc // nt
    tiles = per * 4
    last = nl - 1
    me = lax.axis_index("tier")
    tile = lax.axis_index("tile")
    lane = lax.broadcasted_iota(jnp.int32, (8, 128), 1)
    sub = lax.broadcasted_iota(jnp.int32, (8, 128), 0)
    first_lane = lane == 0
    last_lane = lane == 127

    groups = ((0, 2), (nl - 2, nl), (2, nl - 2))
    for g, (a, b) in enumerate(groups):
        for c in range(nc):
            cols = pl.ds(128 * c, 128)
            pltpu.make_async_copy(t_hbm.at[0, pl.ds(a, b - a), :, cols], t0.at[pl.ds(a, b - a), c], load_sem.at[2 * g]).start()
            pltpu.make_async_copy(lab_hbm.at[0, pl.ds(a, b - a), :, cols], lab.at[pl.ds(a, b - a), c], load_sem.at[2 * g + 1]).start()
        if g == 1:
            for c in range(nc):
                cols = pl.ds(128 * c, 128)
                pltpu.make_async_copy(patch_hbm.at[0, :, cols], patch.at[c], load_sem.at[6]).start()
            for c in range(per):
                cols = pl.ds(pl.multiple_of((me * per + c) * 128, 128), 128)
                pltpu.make_async_copy(zone_hbm.at[:, cols], zone.at[c], load_sem.at[7]).start()

    def wait_load(g):
        a, b = groups[g]
        whole = pl.ds(a, b - a)
        pltpu.make_async_copy(t0.at[whole], t0.at[whole], load_sem.at[2 * g]).wait()
        pltpu.make_async_copy(lab.at[whole], lab.at[whole], load_sem.at[2 * g + 1]).wait()

    barrier = pltpu.get_barrier_semaphore()
    for d in range(1, nt):
        pl.semaphore_signal(barrier, inc=1, device_id={"tier": lax.rem(me + d, nt)}, device_id_type=MESH)

    @pl.when(tile > 0)
    def _():
        pl.semaphore_signal(barrier, inc=1, device_id={"tile": tile - 1}, device_id_type=MESH)

    @pl.when(tile < nk - 1)
    def _():
        pl.semaphore_signal(barrier, inc=1, device_id={"tile": tile + 1}, device_id_type=MESH)

    ktable = jnp.broadcast_to(ktab[...], (8, 128))
    stable = jnp.broadcast_to(stab[...], (8, 128))

    def fill_kappa(l):
        for c in range(nc):
            for q in range(4):
                kk[l, c, pl.ds(8 * q, 8), :] = lookup(ktable, lab[l, c, pl.ds(q, 8, stride=4), :])

    def edge_rows(ref, dst, where, l):
        for side, row in ((0, 0), (1, 31)):
            for c in range(0, nc, 8):
                n = min(8, nc - c)
                dst[where + (side, pl.ds(l * nc + c, n), slice(None))] = ref[l, pl.ds(c, n), row, :]

    def halo_copy(send, recv, ssem, rsem, at, sem_at, side, rows):
        return pltpu.make_async_remote_copy(
            src_ref=send.at[at + (side, rows)],
            dst_ref=recv.at[at + (side, rows)],
            send_sem=ssem.at[sem_at + (side,)],
            recv_sem=rsem.at[sem_at + (side,)],
            device_id={"tile": tile - 1 if side == 0 else tile + 1},
            device_id_type=MESH,
        )

    spans = (pl.ds(0, nc), pl.ds(last * nc, nc), pl.ds(nc, (nl - 2) * nc))

    def halos(step, what, start):
        copies = [(hs, hr, hs_sem, hr_sem, (step,), (step, what))]
        if step == 0:
            copies.append((ks, kr, ks_sem, kr_sem, (), (what,)))
        for side in (0, 1):
            sends = (tile > 0) if side == 0 else (tile < nk - 1)
            gets = (tile < nk - 1) if side == 0 else (tile > 0)
            for parts in copies:
                copy = halo_copy(*parts, side, spans[what])
                if start == "start":
                    @pl.when(sends)
                    def _(copy=copy):
                        copy.start()
                elif start == "recv":
                    @pl.when(gets)
                    def _(copy=copy):
                        copy.wait_recv()
                else:
                    @pl.when(sends)
                    def _(copy=copy):
                        copy.wait_send()

    zero_rows = jnp.zeros((nl * nc, 128), F32)

    @pl.when(tile == nk - 1)
    def _():
        for step in range(STEPS):
            hr[step, 0] = zero_rows
        kr[0] = zero_rows

    @pl.when(tile == 0)
    def _():
        for step in range(STEPS):
            hr[step, 1] = zero_rows
        kr[1] = zero_rows

    def layer(step, l, up, down, emit):
        if step == 0:
            def temp(l, c, q):
                return t0[l, c, pl.ds(q, 8, stride=4), :]
        else:
            def temp(l, c, q):
                return t1[l, c, pl.ds(8 * q, 8), :]

        def cond(l, c, q):
            return kk[l, c, pl.ds(8 * q, 8), :]

        zero = jnp.zeros((8, 128), F32)
        t_next = [temp(l, 0, q) for q in range(4)]
        k_next = [cond(l, 0, q) for q in range(4)]
        before = None
        for c in range(nc):
            t, k = t_next, k_next
            if c + 1 < nc:
                t_next = [temp(l, c + 1, q) for q in range(4)]
                k_next = [cond(l, c + 1, q) for q in range(4)]
            else:
                t_next = k_next = [zero] * 4
            row = pl.ds(l * nc + c, 1)
            below_t = jnp.broadcast_to(hr[step, 0, row, :], (8, 128))
            above_t = jnp.broadcast_to(hr[step, 1, row, :], (8, 128))
            below_k = jnp.broadcast_to(kr[0, row, :], (8, 128))
            above_k = jnp.broadcast_to(kr[1, row, :], (8, 128))
            t_down = t[1:] + [jnp.where(sub == 7, below_t, pltpu.roll(t[0], 7, 0))]
            k_down = k[1:] + [jnp.where(sub == 7, below_k, pltpu.roll(k[0], 7, 0))]
            fy = [(k[q] + k_down[q]) * (t_down[q] - t[q]) for q in range(4)]
            over = jnp.where(sub == 0, (k[0] + above_k) * (t[0] - above_t), pltpu.roll(fy[3], 1, 0))
            fx = []
            for q in range(4):
                tr = pltpu.roll(jnp.where(first_lane, t_next[q], t[q]), 127, 1)
                krr = pltpu.roll(jnp.where(first_lane, k_next[q], k[q]), 127, 1)
                fx.append((k[q] + krr) * (tr - t[q]))
            for q in range(4):
                if c == 0:
                    left = jnp.where(first_lane, k[q] * t[q], pltpu.roll(fx[q], 1, 1))
                else:
                    left = pltpu.roll(jnp.where(last_lane, before[q], fx[q]), 1, 1)
                new = t[q] + (fx[q] - left) + (fy[q] - (over if q == 0 else fy[q - 1]))
                if down:
                    new = new + (k[q] + cond(l + 1, c, q)) * (temp(l + 1, c, q) - t[q])
                if up:
                    new = new - (k[q] + cond(l - 1, c, q)) * (t[q] - temp(l - 1, c, q))
                emit(c, q, new)
            before = fx

    def mine(n):
        return pl.ds(pl.multiple_of(n * per, per), per)

    def forward(step, h, d):
        peer = lax.rem(me + d, nt)
        return pltpu.make_async_remote_copy(
            src_ref=planes.at[step, h, mine(peer)],
            dst_ref=rx.at[step, h, me],
            send_sem=fs_sem.at[step, h, d],
            recv_sem=fr_sem.at[step, h, d],
            device_id={"tier": peer},
            device_id_type=MESH,
        )

    def forward_own(step, h):
        return pltpu.make_async_copy(planes.at[step, h, mine(me)], rx.at[step, h, me], own_sem.at[step, h])

    def landing(step, h):
        return t1.at[h * last] if step == 0 else back.at[h]

    def backward(step, h, d):
        peer = lax.rem(me + d, nt)
        return pltpu.make_async_remote_copy(
            src_ref=solved.at[step, h, peer],
            dst_ref=landing(step, h).at[mine(me)],
            send_sem=bs_sem.at[step, h, d],
            recv_sem=br_sem.at[step, h, d],
            device_id={"tier": peer},
            device_id_type=MESH,
        )

    def backward_own(step, h):
        return pltpu.make_async_copy(solved.at[step, h, me], landing(step, h).at[mine(me)], own_sem.at[step, 2 + h])

    order = [d for d in range(1, nt)]

    def boundary(step, h):
        def emit(c, q, new):
            if h == 0:
                new = new + src[c, pl.ds(8 * q, 8), :]
            planes[step, h, c, pl.ds(8 * q, 8), :] = new
        layer(step, h * last, h == 1, h == 0, emit)
        for d in order:
            forward(step, h, d).start()
        forward_own(step, h).start()

    def solve(step):
        for h in (0, 1):
            forward_own(step, h).wait()
            for d in order:
                forward(step, h, d).wait_recv()
            for u in range(tiles):
                p = [rx[step, h, t, u // 4, pl.ds(8 * (u % 4), 8), :] for t in range(nt)]

                @pl.loop(0, 2 * nt)
                def _(i, p=p, u=u):
                    total = coef[i, h, 0, u] * p[0]
                    for t in range(1, nt):
                        total = total + coef[i, h, t, u] * p[t]
                    if h == 0:
                        part[i, u] = total
                    else:
                        solved[step, lax.rem(i, 2), i // 2, u // 4, pl.ds(8 * (u % 4), 8), :] = part[i, u] + total
        for h in (0, 1):
            for d in order:
                backward(step, h, d).start()
            backward_own(step, h).start()

    wait_load(0)
    wait_load(1)
    for l in (0, last):
        fill_kappa(l)
        edge_rows(t0, hs, (0,), l)
        edge_rows(kk, ks, (), l)
    greeted = (nt - 1) + (tile > 0).astype(jnp.int32) + (tile < nk - 1).astype(jnp.int32)
    pl.semaphore_wait(barrier, greeted)
    halos(0, 0, "start")
    halos(0, 1, "start")
    fill_kappa(1)
    fill_kappa(last - 1)
    pltpu.make_async_copy(patch, patch, load_sem.at[6]).wait()
    for c in range(nc):
        for q in range(4):
            src[c, pl.ds(8 * q, 8), :] = lookup(stable, patch[c, pl.ds(q, 8, stride=4), :])
    halos(0, 0, "recv")
    boundary(0, 0)
    halos(0, 1, "recv")
    boundary(0, 1)

    wait_load(2)

    @pl.loop(1, last)
    def _(l):
        fill_kappa(l)
        edge_rows(t0, hs, (0,), l)
        edge_rows(kk, ks, (), l)

    halos(0, 2, "start")

    pltpu.make_async_copy(zone, zone, load_sem.at[7]).wait()
    zones = [zone[u // 4, pl.ds(u % 4, 8, stride=4), :] for u in range(tiles)]

    @pl.loop(0, 2 * nt)
    def _(i):
        table = jnp.broadcast_to(mtab[pl.ds(i, 1), :], (8, 128))
        for t in range(nt):
            for h in (0, 1):
                for u in range(tiles):
                    coef[i, h, t, u] = lookup(table, zones[u] + (2 * t + h) * regions)

    halos(0, 2, "recv")

    def inner(step, l, dst):
        def emit(c, q, new):
            if step == 0:
                dst[l, c, pl.ds(8 * q, 8), :] = new
            else:
                dst[l, c, pl.ds(q, 8, stride=4), :] = new
        layer(step, l, True, True, emit)

    @pl.loop(1, last)
    def _(l):
        inner(0, l, t1)
        edge_rows(t1, hs, (1,), l)

    halos(1, 2, "start")
    solve(0)

    halos(1, 2, "recv")

    @pl.loop(2, last - 1)
    def _(l):
        inner(1, l, t2)

    def put(a, n):
        whole = pl.ds(a, n)
        return [
            pltpu.make_async_copy(t2.at[whole, c], out_hbm.at[whole, :, pl.ds(128 * c, 128)], out_sem.at[a])
            for c in range(nc)
        ]

    for copy in put(2, nl - 4):
        copy.start()
    for h in (0, 1):
        backward_own(0, h).wait()
        for d in order:
            backward(0, h, d).wait_recv()
        edge_rows(t1, hs, (1,), h * last)
        halos(1, h, "start")
    for h in (0, 1):
        halos(1, h, "recv")
        boundary(1, h)
    for l in (1, last - 1):
        inner(1, l, t2)
        for copy in put(l, 1):
            copy.start()
    solve(1)
    for h in (0, 1):
        backward_own(1, h).wait()
        for d in order:
            backward(1, h, d).wait_recv()
        for c in range(nc):
            for q in range(4):
                t2[h * last, c, pl.ds(q, 8, stride=4), :] = back[h, c, pl.ds(8 * q, 8), :]
        for copy in put(h * last, 1):
            copy.start()

    for a, n in ((2, nl - 4), (1, 1), (last - 1, 1), (0, 1), (last, 1)):
        whole = pl.ds(a, n)
        pltpu.make_async_copy(t2.at[whole], t2.at[whole], out_sem.at[a]).wait()
    for step in range(STEPS):
        for h in (0, 1):
            for d in order:
                forward(step, h, d).wait_send()
                backward(step, h, d).wait_send()
        for what in range(3):
            halos(step, what, "send")


def make_local(mesh):
    nt, nk = mesh.shape["tier"], mesh.shape["tile"]

    def local(temperature, labels, zones, patches, kappa, power, operators):
        _, nl, rows, cols = temperature.shape
        nc = cols // 128
        regions, block, _ = operators.shape
        dims = (nt, nk, nl, nc, regions)
        per = nc // nt

        def row(x):
            return jnp.pad(x, ((0, 0), (0, 128 - x.shape[1])))

        ktab = row((STEP_DT * 0.5) * kappa[None, :])
        stab = row(STEP_DT * power)
        mtab = row(operators.transpose(1, 2, 0).reshape(block, block * regions))
        any_spec = pl.BlockSpec(memory_space=pl.ANY)
        vmem = pl.BlockSpec(memory_space=pltpu.VMEM)
        dma = pltpu.SemaphoreType.DMA
        out = pl.pallas_call(
            functools.partial(heat_kernel, dims),
            out_shape=jax.ShapeDtypeStruct((nl, rows, cols), F32),
            in_specs=[any_spec] * 4 + [vmem] * 3,
            out_specs=any_spec,
            scratch_shapes=[
                pltpu.VMEM((nl, nc, 32, 128), F32),
                pltpu.VMEM((nl, nc, 32, 128), jnp.int32),
                pltpu.VMEM((nl, nc, 32, 128), F32),
                pltpu.VMEM((nl, nc, 32, 128), F32),
                pltpu.VMEM((nl, nc, 32, 128), F32),
                pltpu.VMEM((per, 32, 128), jnp.int32),
                pltpu.VMEM((nc, 32, 128), jnp.int32),
                pltpu.VMEM((nc, 32, 128), F32),
                pltpu.VMEM((2 * nt, 2, nt, per * 4, 8, 128), F32),
                pltpu.VMEM((STEPS, 2, nc, 32, 128), F32),
                pltpu.VMEM((STEPS, 2, nt, per, 32, 128), F32),
                pltpu.VMEM((2 * nt, per * 4, 8, 128), F32),
                pltpu.VMEM((STEPS, 2, nt, per, 32, 128), F32),
                pltpu.VMEM((2, nc, 32, 128), F32),
                pltpu.VMEM((STEPS, 2, nl * nc, 128), F32),
                pltpu.VMEM((STEPS, 2, nl * nc, 128), F32),
                pltpu.VMEM((2, nl * nc, 128), F32),
                pltpu.VMEM((2, nl * nc, 128), F32),
                dma((8,)),
                dma((nl,)),
                dma((STEPS, 3, 2)),
                dma((STEPS, 3, 2)),
                dma((3, 2)),
                dma((3, 2)),
                dma((STEPS, 2, nt)),
                dma((STEPS, 2, nt)),
                dma((STEPS, 2, nt)),
                dma((STEPS, 2, nt)),
                dma((STEPS, 4)),
            ],
            compiler_params=pltpu.CompilerParams(
                collective_id=0, has_side_effects=True, vmem_limit_bytes=56 * 1024 * 1024
            ),
            name="heat",
        )(temperature, labels, zones, patches, ktab, stab, mtab)
        return out[None]

    return local


def solution(mesh):
    in_specs = (
        P("tier", None, "tile", None),
        P("tier", None, "tile", None),
        P("tile", None),
        P("tier", "tile", None),
        P(),
        P("tier", None),
        P(),
    )
    out_specs = P("tier", None, "tile", None)
    return jax.shard_map(make_local(mesh), mesh=mesh, in_specs=in_specs, out_specs=out_specs, check_vma=False)
```

```python
import functools

import jax
import jax.numpy as jnp
from jax import lax
from jax.experimental import pallas as pl
from jax.experimental.pallas import tpu as pltpu
from jax.sharding import PartitionSpec as P

STEPS = 2
STEP_DT = 0.04
MESH = pl.DeviceIdType.MESH
F32 = jnp.float32


def lookup(table, index):
    return lax.gather(
        table,
        index[..., None],
        lax.GatherDimensionNumbers(
            offset_dims=(), collapsed_slice_dims=(1,), start_index_map=(1,),
            operand_batching_dims=(0,), start_indices_batching_dims=(0,),
        ),
        slice_sizes=(1, 1),
        mode=lax.GatherScatterMode.PROMISE_IN_BOUNDS,
    )


def heat_kernel(
    dims,
    t_hbm, lab_hbm, zone_hbm, patch_hbm, kappa, power, operators,
    t2,
    t0, lab, t1, kk, zone, patch, src, coef, planes, rx, part, solved, back,
    hs, hr, ks, kr, ktab, mtab,
    load_sem, hs_sem, hr_sem, ks_sem, kr_sem,
    fs_sem, fr_sem, bs_sem, br_sem, own_sem,
):
    nt, nk, nl, nc, regions = dims
    per = nc // nt
    tiles = per * 4
    last = nl - 1
    me = lax.axis_index("tier")
    tile = lax.axis_index("tile")
    lane = lax.broadcasted_iota(jnp.int32, (8, 128), 1)
    sub = lax.broadcasted_iota(jnp.int32, (8, 128), 0)
    first_lane = lane == 0
    last_lane = lane == 127

    groups = ((0, 2), (nl - 2, nl), (2, nl - 2))
    for g, (a, b) in enumerate(groups):
        for c in range(nc):
            cols = pl.ds(128 * c, 128)
            pltpu.make_async_copy(t_hbm.at[0, pl.ds(a, b - a), :, cols], t0.at[pl.ds(a, b - a), c], load_sem.at[2 * g]).start()
            pltpu.make_async_copy(lab_hbm.at[0, pl.ds(a, b - a), :, cols], lab.at[pl.ds(a, b - a), c], load_sem.at[2 * g + 1]).start()
        if g == 1:
            for c in range(nc):
                cols = pl.ds(128 * c, 128)
                pltpu.make_async_copy(patch_hbm.at[0, :, cols], patch.at[c], load_sem.at[6]).start()
            for c in range(per):
                cols = pl.ds(pl.multiple_of((me * per + c) * 128, 128), 128)
                pltpu.make_async_copy(zone_hbm.at[:, cols], zone.at[c], load_sem.at[7]).start()

    def wait_load(g):
        a, b = groups[g]
        whole = pl.ds(a, b - a)
        pltpu.make_async_copy(t0.at[whole], t0.at[whole], load_sem.at[2 * g]).wait()
        pltpu.make_async_copy(lab.at[whole], lab.at[whole], load_sem.at[2 * g + 1]).wait()

    barrier = pltpu.get_barrier_semaphore()
    for d in range(1, nt):
        pl.semaphore_signal(barrier, inc=1, device_id={"tier": lax.rem(me + d, nt)}, device_id_type=MESH)

    @pl.when(tile > 0)
    def _():
        pl.semaphore_signal(barrier, inc=1, device_id={"tile": tile - 1}, device_id_type=MESH)

    @pl.when(tile < nk - 1)
    def _():
        pl.semaphore_signal(barrier, inc=1, device_id={"tile": tile + 1}, device_id_type=MESH)

    ktab[...] = jnp.zeros((8, 128), F32)
    ktab[:, 0:kappa.shape[1]] = jnp.broadcast_to((STEP_DT * 0.5) * kappa[...], (8, kappa.shape[1]))
    ktable = ktab[...]
    stable = jnp.broadcast_to(STEP_DT * power[...], (8, 128))
    block = 2 * nt
    for w in range(regions):
        mtab[:, w * block:(w + 1) * block] = operators[w]

    def fill_kappa(l):
        for c in range(nc):
            for q in range(4):
                kk[l, c, pl.ds(8 * q, 8), :] = lookup(ktable, lab[l, c, pl.ds(q, 8, stride=4), :])

    def edge_rows(ref, dst, where, l):
        for side, row in ((0, 0), (1, 31)):
            for c in range(0, nc, 8):
                n = min(8, nc - c)
                dst[where + (side, pl.ds(l * nc + c, n), slice(None))] = ref[l, pl.ds(c, n), row, :]

    def halo_copy(send, recv, ssem, rsem, at, sem_at, side, rows):
        return pltpu.make_async_remote_copy(
            src_ref=send.at[at + (side, rows)],
            dst_ref=recv.at[at + (side, rows)],
            send_sem=ssem.at[sem_at + (side,)],
            recv_sem=rsem.at[sem_at + (side,)],
            device_id={"tile": tile - 1 if side == 0 else tile + 1},
            device_id_type=MESH,
        )

    spans = (pl.ds(0, nc), pl.ds(last * nc, nc), pl.ds(nc, (nl - 2) * nc))

    def halos(step, what, start):
        copies = [(hs, hr, hs_sem, hr_sem, (step,), (step, what))]
        if step == 0:
            copies.append((ks, kr, ks_sem, kr_sem, (), (what,)))
        for side in (0, 1):
            sends = (tile > 0) if side == 0 else (tile < nk - 1)
            gets = (tile < nk - 1) if side == 0 else (tile > 0)
            for parts in copies:
                copy = halo_copy(*parts, side, spans[what])
                if start == "start":
                    @pl.when(sends)
                    def _(copy=copy):
                        copy.start()
                elif start == "recv":
                    @pl.when(gets)
                    def _(copy=copy):
                        copy.wait_recv()
                else:
                    @pl.when(sends)
                    def _(copy=copy):
                        copy.wait_send()

    zero_rows = jnp.zeros((nl * nc, 128), F32)

    @pl.when(tile == nk - 1)
    def _():
        for step in range(STEPS):
            hr[step, 0] = zero_rows
        kr[0] = zero_rows

    @pl.when(tile == 0)
    def _():
        for step in range(STEPS):
            hr[step, 1] = zero_rows
        kr[1] = zero_rows

    def layer(step, l, up, down, emit):
        if step == 0:
            def temp(l, c, q):
                return t0[l, c, pl.ds(q, 8, stride=4), :]
        else:
            def temp(l, c, q):
                return t1[l, c, pl.ds(8 * q, 8), :]

        def cond(l, c, q):
            return kk[l, c, pl.ds(8 * q, 8), :]

        zero = jnp.zeros((8, 128), F32)
        t_next = [temp(l, 0, q) for q in range(4)]
        k_next = [cond(l, 0, q) for q in range(4)]
        before = None
        for c in range(nc):
            t, k = t_next, k_next
            if c + 1 < nc:
                t_next = [temp(l, c + 1, q) for q in range(4)]
                k_next = [cond(l, c + 1, q) for q in range(4)]
            else:
                t_next = k_next = [zero] * 4
            row = pl.ds(l * nc + c, 1)
            below_t = jnp.broadcast_to(hr[step, 0, row, :], (8, 128))
            above_t = jnp.broadcast_to(hr[step, 1, row, :], (8, 128))
            below_k = jnp.broadcast_to(kr[0, row, :], (8, 128))
            above_k = jnp.broadcast_to(kr[1, row, :], (8, 128))
            t_down = t[1:] + [jnp.where(sub == 7, below_t, pltpu.roll(t[0], 7, 0))]
            k_down = k[1:] + [jnp.where(sub == 7, below_k, pltpu.roll(k[0], 7, 0))]
            fy = [(k[q] + k_down[q]) * (t_down[q] - t[q]) for q in range(4)]
            over = jnp.where(sub == 0, (k[0] + above_k) * (t[0] - above_t), pltpu.roll(fy[3], 1, 0))
            fx = []
            for q in range(4):
                tr = pltpu.roll(jnp.where(first_lane, t_next[q], t[q]), 127, 1)
                krr = pltpu.roll(jnp.where(first_lane, k_next[q], k[q]), 127, 1)
                fx.append((k[q] + krr) * (tr - t[q]))
            for q in range(4):
                if c == 0:
                    left = jnp.where(first_lane, k[q] * t[q], pltpu.roll(fx[q], 1, 1))
                else:
                    left = pltpu.roll(jnp.where(last_lane, before[q], fx[q]), 1, 1)
                new = t[q] + (fx[q] - left) + (fy[q] - (over if q == 0 else fy[q - 1]))
                if down:
                    new = new + (k[q] + cond(l + 1, c, q)) * (temp(l + 1, c, q) - t[q])
                if up:
                    new = new - (k[q] + cond(l - 1, c, q)) * (t[q] - temp(l - 1, c, q))
                emit(c, q, new)
            before = fx

    def mine(n):
        return pl.ds(pl.multiple_of(n * per, per), per)

    def forward(step, h, d):
        peer = lax.rem(me + d, nt)
        return pltpu.make_async_remote_copy(
            src_ref=planes.at[step, h, mine(peer)],
            dst_ref=rx.at[step, h, me],
            send_sem=fs_sem.at[step, h, d],
            recv_sem=fr_sem.at[step, h, d],
            device_id={"tier": peer},
            device_id_type=MESH,
        )

    def forward_own(step, h):
        return pltpu.make_async_copy(planes.at[step, h, mine(me)], rx.at[step, h, me], own_sem.at[step, h])

    def landing(step, h):
        return t1.at[h * last] if step == 0 else back.at[h]

    def backward(step, h, d):
        peer = lax.rem(me + d, nt)
        return pltpu.make_async_remote_copy(
            src_ref=solved.at[step, h, peer],
            dst_ref=landing(step, h).at[mine(me)],
            send_sem=bs_sem.at[step, h, d],
            recv_sem=br_sem.at[step, h, d],
            device_id={"tier": peer},
            device_id_type=MESH,
        )

    def backward_own(step, h):
        return pltpu.make_async_copy(solved.at[step, h, me], landing(step, h).at[mine(me)], own_sem.at[step, 2 + h])

    order = [d for d in range(1, nt)]

    def boundary(step, h):
        def emit(c, q, new):
            if h == 0:
                new = new + src[c, pl.ds(8 * q, 8), :]
            planes[step, h, c, pl.ds(8 * q, 8), :] = new
        layer(step, h * last, h == 1, h == 0, emit)
        for d in order:
            forward(step, h, d).start()
        forward_own(step, h).start()

    def solve(step):
        for h in (0, 1):
            forward_own(step, h).wait()
            for d in order:
                forward(step, h, d).wait_recv()
            @pl.loop(0, tiles)
            def _(u):
                where = (u // 4, pl.ds(pl.multiple_of(8 * lax.rem(u, 4), 8), 8), slice(None))
                p = [rx[(step, h, t) + where] for t in range(nt)]
                for i in range(block):
                    terms = [coef[i, h, t, u] * p[t] for t in range(nt)]
                    if h == 1:
                        terms.append(part[i, u])
                    while len(terms) > 1:
                        terms = [a + b for a, b in zip(terms[::2], terms[1::2])] + terms[len(terms) & ~1:]
                    if h == 0:
                        part[i, u] = terms[0]
                    else:
                        solved[(step, i % 2, i // 2) + where] = terms[0]
        for h in (0, 1):
            for d in order:
                backward(step, h, d).start()
            backward_own(step, h).start()

    wait_load(0)
    wait_load(1)
    for l in (0, last):
        fill_kappa(l)
        edge_rows(t0, hs, (0,), l)
        edge_rows(kk, ks, (), l)
    greeted = (nt - 1) + (tile > 0).astype(jnp.int32) + (tile < nk - 1).astype(jnp.int32)
    pl.semaphore_wait(barrier, greeted)
    halos(0, 0, "start")
    halos(0, 1, "start")
    fill_kappa(1)
    fill_kappa(last - 1)
    pltpu.make_async_copy(patch, patch, load_sem.at[6]).wait()
    for c in range(nc):
        for q in range(4):
            src[c, pl.ds(8 * q, 8), :] = lookup(stable, patch[c, pl.ds(q, 8, stride=4), :])
    halos(0, 0, "recv")
    boundary(0, 0)
    halos(0, 1, "recv")
    boundary(0, 1)

    wait_load(2)

    @pl.loop(1, last)
    def _(l):
        fill_kappa(l)
        edge_rows(t0, hs, (0,), l)
        edge_rows(kk, ks, (), l)

    halos(0, 2, "start")

    pltpu.make_async_copy(zone, zone, load_sem.at[7]).wait()
    zones = [zone[u // 4, pl.ds(u % 4, 8, stride=4), :] * block for u in range(tiles)]

    @pl.loop(0, 2 * nt)
    def _(i):
        table = jnp.broadcast_to(mtab[pl.ds(i, 1), :], (8, 128))
        for t in range(nt):
            for h in (0, 1):
                for u in range(tiles):
                    coef[i, h, t, u] = lookup(table, zones[u] + (2 * t + h))

    solve(0)
    halos(0, 2, "recv")

    def inner(step, l, dst):
        def emit(c, q, new):
            if step == 0:
                dst[l, c, pl.ds(8 * q, 8), :] = new
            else:
                dst[l, c, pl.ds(q, 8, stride=4), :] = new
        layer(step, l, True, True, emit)

    @pl.loop(1, last)
    def _(l):
        inner(0, l, t1)
        edge_rows(t1, hs, (1,), l)

    halos(1, 2, "start")

    for h in (0, 1):
        backward_own(0, h).wait()
        for d in order:
            backward(0, h, d).wait_recv()
        edge_rows(t1, hs, (1,), h * last)
        halos(1, h, "start")
    for h in (0, 1):
        halos(1, h, "recv")
        boundary(1, h)
    halos(1, 2, "recv")

    @pl.loop(2, last - 1)
    def _(l):
        inner(1, l, t2)

    solve(1)
    for l in (1, last - 1):
        inner(1, l, t2)
    for h in (0, 1):
        backward_own(1, h).wait()
        for d in order:
            backward(1, h, d).wait_recv()
        for c in range(nc):
            for q in range(4):
                t2[h * last, c, pl.ds(q, 8, stride=4), :] = back[h, c, pl.ds(8 * q, 8), :]

    for step in range(STEPS):
        for h in (0, 1):
            for d in order:
                forward(step, h, d).wait_send()
                backward(step, h, d).wait_send()
        for what in range(3):
            halos(step, what, "send")


def put_kernel(source, out, sem):
    copies = [
        pltpu.make_async_copy(source.at[:, c], out.at[:, :, pl.ds(128 * c, 128)], sem)
        for c in range(source.shape[1])
    ]
    for copy in copies:
        copy.start()
    pltpu.make_async_copy(source, source, sem).wait()


def make_local(mesh):
    nt, nk = mesh.shape["tier"], mesh.shape["tile"]

    def local(temperature, labels, zones, patches, kappa, power, operators):
        _, nl, rows, cols = temperature.shape
        nc = cols // 128
        regions, block, _ = operators.shape
        dims = (nt, nk, nl, nc, regions)
        per = nc // nt

        any_spec = pl.BlockSpec(memory_space=pl.ANY)
        vmem = pl.BlockSpec(memory_space=pltpu.VMEM)
        dma = pltpu.SemaphoreType.DMA
        out = pl.pallas_call(
            functools.partial(heat_kernel, dims),
            out_shape=pltpu.VMEM((nl, nc, 32, 128), F32),
            in_specs=[any_spec] * 4 + [vmem] * 3,
            out_specs=vmem,
            scratch_shapes=[
                pltpu.VMEM((nl, nc, 32, 128), F32),
                pltpu.VMEM((nl, nc, 32, 128), jnp.int32),
                pltpu.VMEM((nl, nc, 32, 128), F32),
                pltpu.VMEM((nl, nc, 32, 128), F32),
                pltpu.VMEM((per, 32, 128), jnp.int32),
                pltpu.VMEM((nc, 32, 128), jnp.int32),
                pltpu.VMEM((nc, 32, 128), F32),
                pltpu.VMEM((2 * nt, 2, nt, per * 4, 8, 128), F32),
                pltpu.VMEM((STEPS, 2, nc, 32, 128), F32),
                pltpu.VMEM((STEPS, 2, nt, per, 32, 128), F32),
                pltpu.VMEM((2 * nt, per * 4, 8, 128), F32),
                pltpu.VMEM((STEPS, 2, nt, per, 32, 128), F32),
                pltpu.VMEM((2, nc, 32, 128), F32),
                pltpu.VMEM((STEPS, 2, nl * nc, 128), F32),
                pltpu.VMEM((STEPS, 2, nl * nc, 128), F32),
                pltpu.VMEM((2, nl * nc, 128), F32),
                pltpu.VMEM((2, nl * nc, 128), F32),
                pltpu.VMEM((8, 128), F32),
                pltpu.VMEM((block, 128), F32),
                dma((8,)),
                dma((STEPS, 3, 2)),
                dma((STEPS, 3, 2)),
                dma((3, 2)),
                dma((3, 2)),
                dma((STEPS, 2, nt)),
                dma((STEPS, 2, nt)),
                dma((STEPS, 2, nt)),
                dma((STEPS, 2, nt)),
                dma((STEPS, 4)),
            ],
            compiler_params=pltpu.CompilerParams(
                collective_id=0, has_side_effects=True, vmem_limit_bytes=62_800_000
            ),
            name="heat",
        )(temperature, labels, zones, patches, kappa[None], power, operators)
        out = pl.pallas_call(
            put_kernel,
            out_shape=jax.ShapeDtypeStruct((nl, rows, cols), F32),
            in_specs=[any_spec],
            out_specs=any_spec,
            scratch_shapes=[dma],
            compiler_params=pltpu.CompilerParams(vmem_limit_bytes=1024 * 1024),
            name="put",
        )(out)
        return out[None]

    return local


def solution(mesh):
    in_specs = (
        P("tier", None, "tile", None),
        P("tier", None, "tile", None),
        P("tile", None),
        P("tier", "tile", None),
        P(),
        P("tier", None),
        P(),
    )
    out_specs = P("tier", None, "tile", None)
    return jax.shard_map(make_local(mesh), mesh=mesh, in_specs=in_specs, out_specs=out_specs, check_vma=False)
```

```python
import functools

import jax
import jax.numpy as jnp
from jax import lax
from jax.experimental import pallas as pl
from jax.experimental.pallas import tpu as pltpu
from jax.sharding import PartitionSpec as P

STEPS = 2
GROUP = (0, 2, 3, 1)
STEP_DT = 0.04
MESH = pl.DeviceIdType.MESH
F32 = jnp.float32


def group(q):
    return pl.ds(8 * GROUP[q], 8)


def lookup(table, index):
    return lax.gather(
        table,
        index[..., None],
        lax.GatherDimensionNumbers(
            offset_dims=(), collapsed_slice_dims=(1,), start_index_map=(1,),
            operand_batching_dims=(0,), start_indices_batching_dims=(0,),
        ),
        slice_sizes=(1, 1),
        mode=lax.GatherScatterMode.PROMISE_IN_BOUNDS,
    )


def heat_kernel(
    dims,
    t_hbm, lab_hbm, zone_hbm, patch_hbm, kappa_hbm, power_hbm, operators_hbm,
    t2,
    t0, lab, t1, kk, zone, patch, src, coef, planes, rx, solved,
    hs, hr, ks, kr, ls, lr, ktab, mtab, em, pe, re, he, ha, back, kappa, power, operators,
    load_sem, table_sem, hs_sem, hr_sem, ks_sem, kr_sem,
    fs_sem, fr_sem, bs_sem, br_sem, own_sem, es_sem, er_sem, as_sem, ar_sem,
):
    nt, nk, nl, nc, regions = dims
    per = nc // nt
    tiles = per * 4
    last = nl - 1
    me = lax.axis_index("tier")
    tile = lax.axis_index("tile")
    lane = lax.broadcasted_iota(jnp.int32, (8, 128), 1)
    sub = lax.broadcasted_iota(jnp.int32, (8, 128), 0)
    first_lane = lane == 0
    last_lane = lane == 127

    barrier = pltpu.get_barrier_semaphore()
    for d in range(1, nt):
        pl.semaphore_signal(barrier, inc=1, device_id={"tier": lax.rem(me + d, nt)}, device_id_type=MESH)

    @pl.when(tile > 0)
    def _():
        pl.semaphore_signal(barrier, inc=1, device_id={"tile": tile - 1}, device_id_type=MESH)

    @pl.when(tile < nk - 1)
    def _():
        pl.semaphore_signal(barrier, inc=1, device_id={"tile": tile + 1}, device_id_type=MESH)

    groups = ((0, 2), (nl - 2, nl), (2, nl - 2))

    def start_load(g):
        a, b = groups[g]
        for c in range(nc):
            cols = pl.ds(128 * c, 128)
            pltpu.make_async_copy(lab_hbm.at[0, pl.ds(a, b - a), :, cols], lab.at[pl.ds(a, b - a), c], load_sem.at[2 * g + 1]).start()
        for c in range(nc):
            cols = pl.ds(128 * c, 128)
            pltpu.make_async_copy(t_hbm.at[0, pl.ds(a, b - a), :, cols], t0.at[pl.ds(a, b - a), c], load_sem.at[2 * g]).start()

    def wait_load(g, labels):
        a, b = groups[g]
        whole = pl.ds(a, b - a)
        if labels:
            pltpu.make_async_copy(lab.at[whole], lab.at[whole], load_sem.at[2 * g + 1]).wait()
        else:
            pltpu.make_async_copy(t0.at[whole], t0.at[whole], load_sem.at[2 * g]).wait()

    tables = [
        pltpu.make_async_copy(kappa_hbm, kappa, table_sem.at[0]),
        pltpu.make_async_copy(power_hbm, power, table_sem.at[1]),
        pltpu.make_async_copy(operators_hbm, operators, table_sem.at[2]),
    ]
    for copy in tables:
        copy.start()
    start_load(0)
    for c in range(nc):
        cols = pl.ds(128 * c, 128)
        pltpu.make_async_copy(patch_hbm.at[0, :, cols], patch.at[c], load_sem.at[6]).start()
    start_load(1)
    for c in range(per):
        cols = pl.ds(pl.multiple_of((me * per + c) * 128, 128), 128)
        pltpu.make_async_copy(zone_hbm.at[:, cols], zone.at[c], load_sem.at[7]).start()
    start_load(2)

    for copy in tables:
        copy.wait()
    ktab[...] = jnp.zeros((8, 128), F32)
    ktab[:, 0:kappa.shape[1]] = jnp.broadcast_to((STEP_DT * 0.5) * kappa[...], (8, kappa.shape[1]))
    ktable = ktab[...]
    stable = jnp.broadcast_to(STEP_DT * power[...], (8, 128))
    block = 2 * nt
    for w in range(regions):
        mtab[:, w * block:(w + 1) * block] = operators[w]

    def fill_kappa(l):
        for c in range(nc):
            for q in range(4):
                kk[l, c, group(q), :] = lookup(ktable, lab[l, c, pl.ds(q, 8, stride=4), :])

    def edge_rows(ref, dst, where, l, far=15):
        for side, row in ((0, 0), (1, far)):
            for c in range(0, nc, 8):
                n = min(8, nc - c)
                dst[where + (side, pl.ds(l * nc + c, n), slice(None))] = ref[l, pl.ds(c, n), row, :]

    def halo_copy(send, recv, ssem, rsem, at, sem_at, side, rows):
        return pltpu.make_async_remote_copy(
            src_ref=send.at[at + (side, rows)],
            dst_ref=recv.at[at + (side, rows)],
            send_sem=ssem.at[sem_at + (side,)],
            recv_sem=rsem.at[sem_at + (side,)],
            device_id={"tile": tile - 1 if side == 0 else tile + 1},
            device_id_type=MESH,
        )

    cut = last // 2
    cut2 = cut + (last - 1 - cut) // 2
    spans = (
        pl.ds(0, nc), pl.ds(last * nc, nc),
        (pl.ds(nc, (nl - 2) * nc), pl.ds(nc, cut * nc)),
        (None, pl.ds((cut + 1) * nc, (last - 1 - cut) * nc)),
    )

    def halos(step, what, start):
        copies = [(hs, hr, hs_sem, hr_sem, (step,), (step, what))]
        if step == 0:
            copies.append((ls, lr, ks_sem, kr_sem, (), (what,)))
        rows = spans[what] if what < 2 else spans[what][step]
        for side in (0, 1):
            sends = (tile > 0) if side == 0 else (tile < nk - 1)
            gets = (tile < nk - 1) if side == 0 else (tile > 0)
            for parts in copies:
                copy = halo_copy(*parts, side, rows)
                if start == "start":
                    @pl.when(sends)
                    def _(copy=copy):
                        copy.start()
                elif start == "recv":
                    @pl.when(gets)
                    def _(copy=copy, labels=parts[1] is lr, side=side):
                        copy.wait_recv()
                        if labels:
                            first, count = rows.start // nc, rows.size // nc

                            @pl.loop(first, first + count)
                            def _(l):
                                for c in range(0, nc, 8):
                                    at = pl.ds(l * nc + c, min(8, nc - c))
                                    kr[side, at, :] = lookup(ktable[:min(8, nc - c)], lr[side, at, :])
                else:
                    @pl.when(sends)
                    def _(copy=copy):
                        copy.wait_send()

    def clear_outside():
        zero_rows = jnp.zeros((nl * nc, 128), F32)

        @pl.when(tile == nk - 1)
        def _():
            for step in range(STEPS):
                hr[step, 0] = zero_rows
            kr[0] = zero_rows
            ha[0] = jnp.zeros((8 * nt, 128), F32)

        @pl.when(tile == 0)
        def _():
            for step in range(STEPS):
                hr[step, 1] = zero_rows
            kr[1] = zero_rows
            ha[1] = jnp.zeros((8 * nt, 128), F32)

    def layer(step, l, up, down, outer, emit):
        if step == 0:
            def temp(l, c, q):
                return t0[l, c, pl.ds(q, 8, stride=4), :]
        else:
            def temp(l, c, q):
                return t1[l, c, group(q), :]

        def cond(l, c, q):
            return kk[l, c, group(q), :]

        zero = jnp.zeros((8, 128), F32)
        t_next = [temp(l, 0, q) for q in range(4)]
        k_next = [cond(l, 0, q) for q in range(4)]
        before = None
        for c in range(nc):
            t, k = t_next, k_next
            if c + 1 < nc:
                t_next = [temp(l, c + 1, q) for q in range(4)]
                k_next = [cond(l, c + 1, q) for q in range(4)]
            else:
                t_next = k_next = [zero] * 4
            if outer:
                row = pl.ds(l * nc + c, 1)
                below_t = jnp.broadcast_to(hr[step, 0, row, :], (8, 128))
                above_t = jnp.broadcast_to(hr[step, 1, row, :], (8, 128))
                below_k = jnp.broadcast_to(kr[0, row, :], (8, 128))
                above_k = jnp.broadcast_to(kr[1, row, :], (8, 128))
                k_down = k[1:] + [jnp.where(sub == 7, below_k, pltpu.roll(k[0], 7, 0))]
            else:
                below_t = t[3]
                k_down = k[1:] + [pltpu.roll(k[0], 7, 0)]
            t_down = t[1:] + [jnp.where(sub == 7, below_t, pltpu.roll(t[0], 7, 0))]
            fy = [(k[q] + k_down[q]) * (t_down[q] - t[q]) for q in range(4)]
            over = pltpu.roll(fy[3], 1, 0)
            if outer:
                over = jnp.where(sub == 0, (k[0] + above_k) * (t[0] - above_t), over)
            fx = []
            for q in range(4):
                tr = pltpu.roll(jnp.where(first_lane, t_next[q], t[q]), 127, 1)
                krr = pltpu.roll(jnp.where(first_lane, k_next[q], k[q]), 127, 1)
                fx.append((k[q] + krr) * (tr - t[q]))
            for q in range(4):
                if c == 0:
                    left = jnp.where(first_lane, k[q] * t[q], pltpu.roll(fx[q], 1, 1))
                else:
                    left = pltpu.roll(jnp.where(last_lane, before[q], fx[q]), 1, 1)
                new = t[q] + (fx[q] - left) + (fy[q] - (over if q == 0 else fy[q - 1]))
                if down:
                    new = new + (k[q] + cond(l + 1, c, q)) * (temp(l + 1, c, q) - t[q])
                if up:
                    new = new - (k[q] + cond(l - 1, c, q)) * (t[q] - temp(l - 1, c, q))
                emit(c, q, new)
            before = fx

    order = [d for d in range(1, nt)]
    chunks = [(h, part) for part in (1, 0) for h in (0, 1)]

    def half(part):
        return pl.ds(16 * part, 16)

    def columns(n):
        return pl.ds(pl.multiple_of(n * per, per), per)

    def forward(step, h, part, d):
        peer = lax.rem(me + d, nt)
        src_ref, dst_ref = planes.at[step, h, columns(peer), half(part)], rx.at[step, h, me, :, half(part)]
        if d == 0:
            return pltpu.make_async_copy(src_ref, dst_ref, own_sem.at[0, step, h, part])
        return pltpu.make_async_remote_copy(
            src_ref=src_ref,
            dst_ref=dst_ref,
            send_sem=fs_sem.at[step, h, part, d],
            recv_sem=fr_sem.at[step, h, part, d],
            device_id={"tier": peer},
            device_id_type=MESH,
        )

    def backward(step, h, part, d):
        peer = lax.rem(me + d, nt)
        landing = t1.at[h * last] if step == 0 else back.at[h]
        src_ref, dst_ref = solved.at[step, h, peer, :, half(part)], landing.at[columns(me), half(part)]
        if d == 0:
            return pltpu.make_async_copy(src_ref, dst_ref, own_sem.at[1, step, h, part])
        return pltpu.make_async_remote_copy(
            src_ref=src_ref,
            dst_ref=dst_ref,
            send_sem=bs_sem.at[step, h, part, d],
            recv_sem=br_sem.at[step, h, part, d],
            device_id={"tier": peer},
            device_id_type=MESH,
        )

    def edge_forward(step, d):
        peer = lax.rem(me + d, nt)
        rows = lambda n: pl.ds(pl.multiple_of(8 * n, 8), 8)
        src_ref, dst_ref = pe.at[step, rows(peer)], re.at[step, rows(me)]
        if d == 0:
            return pltpu.make_async_copy(src_ref, dst_ref, own_sem.at[2, step, 0, 0])
        return pltpu.make_async_remote_copy(
            src_ref=src_ref,
            dst_ref=dst_ref,
            send_sem=es_sem.at[step, d],
            recv_sem=er_sem.at[step, d],
            device_id={"tier": peer},
            device_id_type=MESH,
        )

    def edge_across(side, d):
        peer = lax.rem(me + d, nt)
        rows = lambda n: pl.ds(pl.multiple_of(8 * n, 8), 8)
        return pltpu.make_async_remote_copy(
            src_ref=he.at[rows(peer)],
            dst_ref=ha.at[side, rows(me)],
            send_sem=as_sem.at[side, d],
            recv_sem=ar_sem.at[side, d],
            device_id={"tier": peer, "tile": tile - 1 if side == 0 else tile + 1},
            device_id_type=MESH,
        )

    def edges_across(what):
        for side in (0, 1):
            sends = (tile > 0) if side == 0 else (tile < nk - 1)
            gets = (tile < nk - 1) if side == 0 else (tile > 0)

            @pl.when(gets if what == "recv" else sends)
            def _(side=side):
                for d in range(nt):
                    copy = edge_across(side, d)
                    if what == "start":
                        copy.start()
                    elif what == "recv":
                        copy.wait_recv()
                    else:
                        copy.wait_send()

    def boundary(step, h):
        def emit(c, q, new):
            if h == 0:
                new = new + src[c, group(q), :]
            planes[step, h, c, group(q), :] = new
        layer(step, h * last, h == 1, h == 0, False, emit)

    def send_planes(step):
        for h, part in chunks:
            for d in order + [0]:
                forward(step, h, part, d).start()

    def send_edges(step):
        for h in (0, 1):
            for side, row in ((0, 0), (1, 15)):
                for c in range(0, nc, 8):
                    n = min(8, nc - c)
                    em[h, side, pl.ds(c, n), :] = planes[step, h, pl.ds(c, n), row, :]
        for h in (0, 1):
            for side in (0, 1):
                for cc in range(per):
                    slot = (h * 2 + side) * per + cc
                    rows = pl.ds(h * last * nc + cc, nt, stride=per)
                    if step == 0:
                        th = hr[0, 1 - side, rows, :]
                    else:
                        th = ha[1 - side, pl.ds((h * 2 + 1 - side) * per + cc, nt, stride=8), :]
                    new = em[h, side, pl.ds(cc, nt, stride=per), :]
                    new = new + (ks[side, rows, :] + kr[1 - side, rows, :]) * (th - hs[step, side, rows, :])
                    pe[step, pl.ds(slot, nt, stride=8), :] = new
        for d in order + [0]:
            edge_forward(step, d).start()

    def solve(step, part):
        for h in (0, 1):
            forward(step, h, part, 0).wait()
            for d in order:
                forward(step, h, part, d).wait_recv()
        if part == 0:
            edge_forward(step, 0).wait()
            for d in order:
                edge_forward(step, d).wait_recv()
            for t in range(nt):
                for h in (0, 1):
                    for side, row in ((0, 0), (1, 15)):
                        for cc in range(per):
                            rx[step, h, t, cc, pl.ds(row, 1), :] = re[step, pl.ds(8 * t + (h * 2 + side) * per + cc, 1), :]

        @pl.loop(0, 2 * per)
        def _(n):
            rows = pl.ds(pl.multiple_of(16 * part + 8 * lax.rem(n, 2), 8), 8)
            cc = n // 2
            p = [rx[step, h, t, cc, rows, :] for h in (0, 1) for t in range(nt)]
            for i in range(block):
                terms = [coef[2 * per * part + n, i, j] * p[j] for j in range(block)]
                while len(terms) > 1:
                    terms = [a + b for a, b in zip(terms[::2], terms[1::2])]
                solved[step, i % 2, i // 2, cc, rows, :] = terms[0]

        for h in (0, 1):
            for d in order + [0]:
                backward(step, h, part, d).start()
        if part == 0 and step == 0:
            for t in range(nt):
                for h in (0, 1):
                    for side, row in ((0, 0), (1, 15)):
                        for cc in range(per):
                            he[pl.ds(8 * t + (h * 2 + side) * per + cc, 1), :] = solved[0, h, t, cc, pl.ds(row, 1), :]
            edges_across("start")

    def wait_back(step, part):
        for h in (0, 1):
            backward(step, h, part, 0).wait()
            for d in order:
                backward(step, h, part, d).wait_recv()

    def inner(step, l):
        def emit(c, q, new):
            if step == 0:
                t1[l, c, group(q), :] = new
            else:
                t2[l, c, pl.ds(q, 8, stride=4), :] = new
        layer(step, l, True, True, True, emit)
        if step == 0:
            edge_rows(t1, hs, (1,), l)

    def fill_coefficients(a, b):
        groups_of = [[0, 3], [1, 2]]
        zones = [
            zone[cc, pl.ds(q, 8, stride=4), :] * block
            for part in (0, 1) for cc in range(per) for q in groups_of[part]
        ]

        @pl.loop(a, b)
        def _(i):
            table = jnp.broadcast_to(mtab[pl.ds(i, 1), :], (8, 128))
            for u in range(tiles):
                for t in range(nt):
                    for h in (0, 1):
                        coef[u, i, h * nt + t] = lookup(table, zones[u] + (2 * t + h))

    wait_load(0, True)
    fill_kappa(0)
    fill_kappa(1)
    pltpu.make_async_copy(patch, patch, load_sem.at[6]).wait()
    for c in range(nc):
        for q in range(4):
            src[c, group(q), :] = lookup(stable, patch[c, pl.ds(q, 8, stride=4), :])
    wait_load(0, False)
    boundary(0, 0)
    wait_load(1, True)
    fill_kappa(last)
    fill_kappa(last - 1)
    wait_load(1, False)
    boundary(0, 1)
    for l in (0, last):
        edge_rows(t0, hs, (0,), l, 31)
        edge_rows(lab, ls, (), l, 31)
        edge_rows(kk, ks, (), l)
    pltpu.make_async_copy(zone, zone, load_sem.at[7]).wait()
    fill_coefficients(0, block // 4)
    wait_load(2, True)
    wait_load(2, False)

    @pl.loop(1, last)
    def _(l):
        edge_rows(t0, hs, (0,), l, 31)
        edge_rows(lab, ls, (), l, 31)

    greeted = (nt - 1) + (tile > 0).astype(jnp.int32) + (tile < nk - 1).astype(jnp.int32)
    pl.semaphore_wait(barrier, greeted)
    halos(0, 0, "start")
    halos(0, 1, "start")
    send_planes(0)
    halos(0, 2, "start")
    clear_outside()
    fill_coefficients(block // 4, block)
    halos(0, 0, "recv")
    halos(0, 1, "recv")
    send_edges(0)
    solve(0, 1)

    @pl.loop(2, last - 1)
    def _(l):
        fill_kappa(l)

    solve(0, 0)
    halos(0, 2, "recv")
    inner(0, last - 1)

    @pl.loop(1, cut + 1)
    def _(l):
        inner(0, l)

    halos(1, 2, "start")

    @pl.loop(cut + 1, cut2 + 1)
    def _(l):
        inner(0, l)

    wait_back(0, 1)
    wait_back(0, 0)
    for h in (0, 1):
        boundary(1, h)
    send_planes(1)
    for h in (0, 1):
        edge_rows(t1, hs, (1,), h * last)

    @pl.loop(cut2 + 1, last - 1)
    def _(l):
        inner(0, l)

    edges_across("recv")
    send_edges(1)
    halos(1, 3, "start")
    halos(1, 2, "recv")

    @pl.loop(2, cut + 1)
    def _(l):
        inner(1, l)

    solve(1, 1)
    inner(1, 1)
    solve(1, 0)
    halos(1, 3, "recv")

    @pl.loop(cut + 1, last)
    def _(l):
        inner(1, l)

    for part, qs in ((1, (1, 2)), (0, (0, 3))):
        wait_back(1, part)
        for h in (0, 1):
            for c in range(nc):
                for q in qs:
                    t2[h * last, c, pl.ds(q, 8, stride=4), :] = back[h, c, group(q), :]

    for step in range(STEPS):
        for h, part in chunks:
            for d in order:
                forward(step, h, part, d).wait_send()
                backward(step, h, part, d).wait_send()
        for d in order:
            edge_forward(step, d).wait_send()
    edges_across("send")
    for step, what in ((0, 0), (0, 1), (0, 2), (1, 2), (1, 3)):
        halos(step, what, "send")


def put_kernel(source, out, sem):
    copies = [
        pltpu.make_async_copy(source.at[:, c], out.at[:, :, pl.ds(128 * c, 128)], sem)
        for c in range(source.shape[1])
    ]
    for copy in copies:
        copy.start()
    pltpu.make_async_copy(source, source, sem).wait()


def make_local(mesh):
    nt, nk = mesh.shape["tier"], mesh.shape["tile"]

    def local(temperature, labels, zones, patches, kappa, power, operators):
        _, nl, rows, cols = temperature.shape
        nc = cols // 128
        regions, block, _ = operators.shape
        dims = (nt, nk, nl, nc, regions)
        per = nc // nt

        any_spec = pl.BlockSpec(memory_space=pl.ANY)
        vmem = pl.BlockSpec(memory_space=pltpu.VMEM)
        dma = pltpu.SemaphoreType.DMA
        out = pl.pallas_call(
            functools.partial(heat_kernel, dims),
            out_shape=pltpu.VMEM((nl, nc, 32, 128), F32),
            in_specs=[any_spec] * 7,
            out_specs=vmem,
            scratch_shapes=[
                pltpu.VMEM((nl, nc, 32, 128), F32),
                pltpu.VMEM((nl, nc, 32, 128), jnp.int32),
                pltpu.VMEM((nl, nc, 32, 128), F32),
                pltpu.VMEM((nl, nc, 32, 128), F32),
                pltpu.VMEM((per, 32, 128), jnp.int32),
                pltpu.VMEM((nc, 32, 128), jnp.int32),
                pltpu.VMEM((nc, 32, 128), F32),
                pltpu.VMEM((per * 4, block, block, 8, 128), F32),
                pltpu.VMEM((STEPS, 2, nc, 32, 128), F32),
                pltpu.VMEM((STEPS, 2, nt, per, 32, 128), F32),
                pltpu.VMEM((STEPS, 2, nt, per, 32, 128), F32),
                pltpu.VMEM((STEPS, 2, nl * nc, 128), F32),
                pltpu.VMEM((STEPS, 2, nl * nc, 128), F32),
                pltpu.VMEM((2, nl * nc, 128), F32),
                pltpu.VMEM((2, nl * nc, 128), F32),
                pltpu.VMEM((2, nl * nc, 128), jnp.int32),
                pltpu.VMEM((2, nl * nc, 128), jnp.int32),
                pltpu.VMEM((8, 128), F32),
                pltpu.VMEM((block, 128), F32),
                pltpu.VMEM((2, 2, nc, 128), F32),
                pltpu.VMEM((STEPS, 8 * nt, 128), F32),
                pltpu.VMEM((STEPS, 8 * nt, 128), F32),
                pltpu.VMEM((8 * nt, 128), F32),
                pltpu.VMEM((2, 8 * nt, 128), F32),
                pltpu.VMEM((2, nc, 32, 128), F32),
                pltpu.VMEM((1, kappa.shape[0]), F32),
                pltpu.VMEM((1, power.shape[1]), F32),
                pltpu.VMEM((regions, block, block), F32),
                dma((8,)),
                dma((3,)),
                dma((STEPS, 4, 2)),
                dma((STEPS, 4, 2)),
                dma((3, 2)),
                dma((3, 2)),
                dma((STEPS, 2, 2, nt)),
                dma((STEPS, 2, 2, nt)),
                dma((STEPS, 2, 2, nt)),
                dma((STEPS, 2, 2, nt)),
                dma((3, STEPS, 2, 2)),
                dma((STEPS, nt)),
                dma((STEPS, nt)),
                dma((2, nt)),
                dma((2, nt)),
            ],
            compiler_params=pltpu.CompilerParams(
                collective_id=0, has_side_effects=True, vmem_limit_bytes=62_800_000
            ),
            name="heat",
        )(temperature, labels, zones, patches, kappa[None], power, operators)
        out = pl.pallas_call(
            put_kernel,
            out_shape=jax.ShapeDtypeStruct((nl, rows, cols), F32),
            in_specs=[any_spec],
            out_specs=any_spec,
            scratch_shapes=[dma],
            compiler_params=pltpu.CompilerParams(vmem_limit_bytes=1024 * 1024),
            name="put",
        )(out)
        return out[None]

    return local


def solution(mesh):
    in_specs = (
        P("tier", None, "tile", None),
        P("tier", None, "tile", None),
        P("tile", None),
        P("tier", "tile", None),
        P(),
        P("tier", None),
        P(),
    )
    out_specs = P("tier", None, "tile", None)
    return jax.shard_map(make_local(mesh), mesh=mesh, in_specs=in_specs, out_specs=out_specs, check_vma=False)
```

```python
import functools

import jax
import jax.numpy as jnp
from jax import lax
from jax.experimental import pallas as pl
from jax.experimental.pallas import tpu as pltpu
from jax.sharding import PartitionSpec as P

STEPS = 2
GROUP = (0, 2, 3, 1)
STEP_DT = 0.04
MESH = pl.DeviceIdType.MESH
F32 = jnp.float32


def group(q):
    return pl.ds(8 * GROUP[q], 8)


def lookup(table, index):
    return lax.gather(
        table,
        index[..., None],
        lax.GatherDimensionNumbers(
            offset_dims=(), collapsed_slice_dims=(1,), start_index_map=(1,),
            operand_batching_dims=(0,), start_indices_batching_dims=(0,),
        ),
        slice_sizes=(1, 1),
        mode=lax.GatherScatterMode.PROMISE_IN_BOUNDS,
    )


def heat_kernel(
    dims,
    t_hbm, lab_hbm, zone_hbm, patch_hbm, kappa_hbm, power_hbm, operators_hbm,
    t2,
    t0, lab, t1, kk, zone, patch, src, coef, planes, rx, solved,
    hs, hr, ks, kr, ls, lr, ktab, mtab, em, pe, re, he, ha, back, kappa, power, operators,
    load_sem, table_sem, hs_sem, hr_sem, ks_sem, kr_sem,
    fs_sem, fr_sem, bs_sem, br_sem, own_sem, es_sem, er_sem, as_sem, ar_sem,
):
    nt, nk, nl, nc, regions = dims
    per = nc // nt
    tiles = per * 4
    last = nl - 1
    me = lax.axis_index("tier")
    tile = lax.axis_index("tile")
    lane = lax.broadcasted_iota(jnp.int32, (8, 128), 1)
    sub = lax.broadcasted_iota(jnp.int32, (8, 128), 0)
    first_lane = lane == 0
    last_lane = lane == 127

    barrier = pltpu.get_barrier_semaphore()
    for d in range(1, nt):
        pl.semaphore_signal(barrier, inc=1, device_id={"tier": lax.rem(me + d, nt)}, device_id_type=MESH)

    @pl.when(tile > 0)
    def _():
        pl.semaphore_signal(barrier, inc=1, device_id={"tile": tile - 1}, device_id_type=MESH)

    @pl.when(tile < nk - 1)
    def _():
        pl.semaphore_signal(barrier, inc=1, device_id={"tile": tile + 1}, device_id_type=MESH)

    groups = ((0, 2), (nl - 2, nl), (2, nl - 2))

    def start_load(g):
        a, b = groups[g]
        for c in range(nc):
            cols = pl.ds(128 * c, 128)
            pltpu.make_async_copy(lab_hbm.at[0, pl.ds(a, b - a), :, cols], lab.at[pl.ds(a, b - a), c], load_sem.at[2 * g + 1]).start()
        for c in range(nc):
            cols = pl.ds(128 * c, 128)
            pltpu.make_async_copy(t_hbm.at[0, pl.ds(a, b - a), :, cols], t0.at[pl.ds(a, b - a), c], load_sem.at[2 * g]).start()

    def wait_load(g, labels):
        a, b = groups[g]
        whole = pl.ds(a, b - a)
        if labels:
            pltpu.make_async_copy(lab.at[whole], lab.at[whole], load_sem.at[2 * g + 1]).wait()
        else:
            pltpu.make_async_copy(t0.at[whole], t0.at[whole], load_sem.at[2 * g]).wait()

    tables = [
        pltpu.make_async_copy(kappa_hbm, kappa, table_sem.at[0]),
        pltpu.make_async_copy(power_hbm, power, table_sem.at[1]),
        pltpu.make_async_copy(operators_hbm, operators, table_sem.at[2]),
    ]
    for copy in tables:
        copy.start()
    start_load(0)
    for c in range(nc):
        cols = pl.ds(128 * c, 128)
        pltpu.make_async_copy(patch_hbm.at[0, :, cols], patch.at[c], load_sem.at[6]).start()
    start_load(1)
    for c in range(per):
        cols = pl.ds(pl.multiple_of((me * per + c) * 128, 128), 128)
        pltpu.make_async_copy(zone_hbm.at[:, cols], zone.at[c], load_sem.at[7]).start()

    for copy in tables:
        copy.wait()
    ktab[...] = jnp.zeros((8, 128), F32)
    ktab[:, 0:kappa.shape[1]] = jnp.broadcast_to((STEP_DT * 0.5) * kappa[...], (8, kappa.shape[1]))
    ktable = ktab[...]
    stable = jnp.broadcast_to(STEP_DT * power[...], (8, 128))
    block = 2 * nt
    for w in range(regions):
        mtab[:, w * block:(w + 1) * block] = operators[w]

    def fill_kappa(l):
        for c in range(nc):
            for q in range(4):
                kk[l, c, group(q), :] = lookup(ktable, lab[l, c, pl.ds(q, 8, stride=4), :])

    def edge_rows(ref, dst, where, l, far=15):
        for side, row in ((0, 0), (1, far)):
            for c in range(0, nc, 8):
                n = min(8, nc - c)
                dst[where + (side, pl.ds(l * nc + c, n), slice(None))] = ref[l, pl.ds(c, n), row, :]

    def halo_copy(send, recv, ssem, rsem, at, sem_at, side, rows):
        return pltpu.make_async_remote_copy(
            src_ref=send.at[at + (side, rows)],
            dst_ref=recv.at[at + (side, rows)],
            send_sem=ssem.at[sem_at + (side,)],
            recv_sem=rsem.at[sem_at + (side,)],
            device_id={"tile": tile - 1 if side == 0 else tile + 1},
            device_id_type=MESH,
        )

    cut = last // 2
    cut2 = cut + (last - 1 - cut) // 2
    cut0 = (cut + 1) // 2

    def layers(a, b):
        return pl.ds(a * nc, (b - a) * nc)

    ends = (layers(0, 1), layers(last, last + 1))
    spans = (
        ends + (layers(1, cut0 + 1), layers(cut0 + 1, cut + 1), layers(cut + 1, cut2 + 1), layers(cut2 + 1, last)),
        ends + (layers(1, cut + 1), layers(cut + 1, last)),
    )

    def halos(step, what, start):
        copies = [(hs, hr, hs_sem, hr_sem, (step,), (step, what))]
        if step == 0:
            copies.append((ls, lr, ks_sem, kr_sem, (), (what,)))
        rows = spans[step][what]
        for side in (0, 1):
            sends = (tile > 0) if side == 0 else (tile < nk - 1)
            gets = (tile < nk - 1) if side == 0 else (tile > 0)
            for parts in copies:
                copy = halo_copy(*parts, side, rows)
                if start == "start":
                    @pl.when(sends)
                    def _(copy=copy):
                        copy.start()
                elif start == "recv":
                    @pl.when(gets)
                    def _(copy=copy, labels=parts[1] is lr, side=side):
                        copy.wait_recv()
                        if labels:
                            first, count = rows.start // nc, rows.size // nc

                            @pl.loop(first, first + count)
                            def _(l):
                                for c in range(0, nc, 8):
                                    at = pl.ds(l * nc + c, min(8, nc - c))
                                    kr[side, at, :] = lookup(ktable[:min(8, nc - c)], lr[side, at, :])
                else:
                    @pl.when(sends)
                    def _(copy=copy):
                        copy.wait_send()

    def clear_outside():
        zero_rows = jnp.zeros((nl * nc, 128), F32)

        @pl.when(tile == nk - 1)
        def _():
            for step in range(STEPS):
                hr[step, 0] = zero_rows
            kr[0] = zero_rows
            ha[0] = jnp.zeros((8 * nt, 128), F32)

        @pl.when(tile == 0)
        def _():
            for step in range(STEPS):
                hr[step, 1] = zero_rows
            kr[1] = zero_rows
            ha[1] = jnp.zeros((8 * nt, 128), F32)

    def layer(step, l, up, down, outer, emit):
        if step == 0:
            def temp(l, c, q):
                return t0[l, c, pl.ds(q, 8, stride=4), :]
        else:
            def temp(l, c, q):
                return t1[l, c, group(q), :]

        def cond(l, c, q):
            return kk[l, c, group(q), :]

        zero = jnp.zeros((8, 128), F32)
        t_next = [temp(l, 0, q) for q in range(4)]
        k_next = [cond(l, 0, q) for q in range(4)]
        before = None
        for c in range(nc):
            t, k = t_next, k_next
            if c + 1 < nc:
                t_next = [temp(l, c + 1, q) for q in range(4)]
                k_next = [cond(l, c + 1, q) for q in range(4)]
            else:
                t_next = k_next = [zero] * 4
            if outer:
                row = pl.ds(l * nc + c, 1)
                below_t = jnp.broadcast_to(hr[step, 0, row, :], (8, 128))
                above_t = jnp.broadcast_to(hr[step, 1, row, :], (8, 128))
                below_k = jnp.broadcast_to(kr[0, row, :], (8, 128))
                above_k = jnp.broadcast_to(kr[1, row, :], (8, 128))
                k_down = k[1:] + [jnp.where(sub == 7, below_k, pltpu.roll(k[0], 7, 0))]
            else:
                below_t = t[3]
                k_down = k[1:] + [pltpu.roll(k[0], 7, 0)]
            t_down = t[1:] + [jnp.where(sub == 7, below_t, pltpu.roll(t[0], 7, 0))]
            fy = [(k[q] + k_down[q]) * (t_down[q] - t[q]) for q in range(4)]
            over = pltpu.roll(fy[3], 1, 0)
            if outer:
                over = jnp.where(sub == 0, (k[0] + above_k) * (t[0] - above_t), over)
            fx = []
            for q in range(4):
                tr = pltpu.roll(jnp.where(first_lane, t_next[q], t[q]), 127, 1)
                krr = pltpu.roll(jnp.where(first_lane, k_next[q], k[q]), 127, 1)
                fx.append((k[q] + krr) * (tr - t[q]))
            for q in range(4):
                if c == 0:
                    left = jnp.where(first_lane, k[q] * t[q], pltpu.roll(fx[q], 1, 1))
                else:
                    left = pltpu.roll(jnp.where(last_lane, before[q], fx[q]), 1, 1)
                new = t[q] + (fx[q] - left) + (fy[q] - (over if q == 0 else fy[q - 1]))
                if down:
                    new = new + (k[q] + cond(l + 1, c, q)) * (temp(l + 1, c, q) - t[q])
                if up:
                    new = new - (k[q] + cond(l - 1, c, q)) * (t[q] - temp(l - 1, c, q))
                emit(c, q, new)
            before = fx

    order = [d for d in range(1, nt)]
    chunks = [(h, part) for part in (1, 0) for h in (0, 1)]

    def half(part):
        return pl.ds(16 * part, 16)

    def columns(n):
        return pl.ds(pl.multiple_of(n * per, per), per)

    def forward(step, h, part, d):
        peer = lax.rem(me + d, nt)
        src_ref, dst_ref = planes.at[step, h, columns(peer), half(part)], rx.at[step, h, me, :, half(part)]
        if d == 0:
            return pltpu.make_async_copy(src_ref, dst_ref, own_sem.at[0, step, h, part])
        return pltpu.make_async_remote_copy(
            src_ref=src_ref,
            dst_ref=dst_ref,
            send_sem=fs_sem.at[step, h, part, d],
            recv_sem=fr_sem.at[step, h, part, d],
            device_id={"tier": peer},
            device_id_type=MESH,
        )

    def backward(step, h, part, d):
        peer = lax.rem(me + d, nt)
        landing = t1.at[h * last] if step == 0 else back.at[h]
        src_ref, dst_ref = solved.at[step, h, peer, :, half(part)], landing.at[columns(me), half(part)]
        if d == 0:
            return pltpu.make_async_copy(src_ref, dst_ref, own_sem.at[1, step, h, part])
        return pltpu.make_async_remote_copy(
            src_ref=src_ref,
            dst_ref=dst_ref,
            send_sem=bs_sem.at[step, h, part, d],
            recv_sem=br_sem.at[step, h, part, d],
            device_id={"tier": peer},
            device_id_type=MESH,
        )

    def edge_forward(step, d):
        peer = lax.rem(me + d, nt)
        rows = lambda n: pl.ds(pl.multiple_of(8 * n, 8), 8)
        src_ref, dst_ref = pe.at[step, rows(peer)], re.at[step, rows(me)]
        if d == 0:
            return pltpu.make_async_copy(src_ref, dst_ref, own_sem.at[2, step, 0, 0])
        return pltpu.make_async_remote_copy(
            src_ref=src_ref,
            dst_ref=dst_ref,
            send_sem=es_sem.at[step, d],
            recv_sem=er_sem.at[step, d],
            device_id={"tier": peer},
            device_id_type=MESH,
        )

    def edge_across(side, d):
        peer = lax.rem(me + d, nt)
        rows = lambda n: pl.ds(pl.multiple_of(8 * n, 8), 8)
        return pltpu.make_async_remote_copy(
            src_ref=he.at[rows(peer)],
            dst_ref=ha.at[side, rows(me)],
            send_sem=as_sem.at[side, d],
            recv_sem=ar_sem.at[side, d],
            device_id={"tier": peer, "tile": tile - 1 if side == 0 else tile + 1},
            device_id_type=MESH,
        )

    def edges_across(what):
        for side in (0, 1):
            sends = (tile > 0) if side == 0 else (tile < nk - 1)
            gets = (tile < nk - 1) if side == 0 else (tile > 0)

            @pl.when(gets if what == "recv" else sends)
            def _(side=side):
                for d in range(nt):
                    copy = edge_across(side, d)
                    if what == "start":
                        copy.start()
                    elif what == "recv":
                        copy.wait_recv()
                    else:
                        copy.wait_send()

    def boundary(step, h):
        def emit(c, q, new):
            if h == 0:
                new = new + src[c, group(q), :]
            planes[step, h, c, group(q), :] = new
        layer(step, h * last, h == 1, h == 0, False, emit)

    def send_planes(step, h):
        for part in (1, 0):
            for d in order + [0]:
                forward(step, h, part, d).start()

    def send_edges(step):
        for h in (0, 1):
            for side, row in ((0, 0), (1, 15)):
                for c in range(0, nc, 8):
                    n = min(8, nc - c)
                    em[h, side, pl.ds(c, n), :] = planes[step, h, pl.ds(c, n), row, :]
        for h in (0, 1):
            for side in (0, 1):
                for cc in range(per):
                    slot = (h * 2 + side) * per + cc
                    rows = pl.ds(h * last * nc + cc, nt, stride=per)
                    if step == 0:
                        th = hr[0, 1 - side, rows, :]
                    else:
                        th = ha[1 - side, pl.ds((h * 2 + 1 - side) * per + cc, nt, stride=8), :]
                    new = em[h, side, pl.ds(cc, nt, stride=per), :]
                    new = new + (ks[side, rows, :] + kr[1 - side, rows, :]) * (th - hs[step, side, rows, :])
                    pe[step, pl.ds(slot, nt, stride=8), :] = new
        for d in order + [0]:
            edge_forward(step, d).start()

    def solve(step, part):
        for h in (0, 1):
            forward(step, h, part, 0).wait()
            for d in order:
                forward(step, h, part, d).wait_recv()
        if part == 0:
            edge_forward(step, 0).wait()
            for d in order:
                edge_forward(step, d).wait_recv()
            for t in range(nt):
                for h in (0, 1):
                    for side, row in ((0, 0), (1, 15)):
                        for cc in range(per):
                            rx[step, h, t, cc, pl.ds(row, 1), :] = re[step, pl.ds(8 * t + (h * 2 + side) * per + cc, 1), :]

        @pl.loop(0, 2 * per)
        def _(n):
            rows = pl.ds(pl.multiple_of(16 * part + 8 * lax.rem(n, 2), 8), 8)
            cc = n // 2
            p = [rx[step, h, t, cc, rows, :] for h in (0, 1) for t in range(nt)]
            for i in range(block):
                terms = [coef[2 * per * part + n, i, j] * p[j] for j in range(block)]
                while len(terms) > 1:
                    terms = [a + b for a, b in zip(terms[::2], terms[1::2])]
                solved[step, i % 2, i // 2, cc, rows, :] = terms[0]

        for h in (0, 1):
            for d in order + [0]:
                backward(step, h, part, d).start()
        if part == 0 and step == 0:
            for t in range(nt):
                for h in (0, 1):
                    for side, row in ((0, 0), (1, 15)):
                        for cc in range(per):
                            he[pl.ds(8 * t + (h * 2 + side) * per + cc, 1), :] = solved[0, h, t, cc, pl.ds(row, 1), :]
            edges_across("start")

    def wait_back(step, h, part):
        backward(step, h, part, 0).wait()
        for d in order:
            backward(step, h, part, d).wait_recv()

    def inner(step, l):
        def emit(c, q, new):
            if step == 0:
                t1[l, c, group(q), :] = new
            else:
                t2[l, c, pl.ds(q, 8, stride=4), :] = new
        layer(step, l, True, True, True, emit)
        if step == 0:
            edge_rows(t1, hs, (1,), l)

    def fill_coefficients(a, b):
        groups_of = [[0, 3], [1, 2]]
        zones = [
            zone[cc, pl.ds(q, 8, stride=4), :] * block
            for part in (0, 1) for cc in range(per) for q in groups_of[part]
        ]

        @pl.loop(a, b)
        def _(i):
            table = jnp.broadcast_to(mtab[pl.ds(i, 1), :], (8, 128))
            for u in range(tiles):
                for t in range(nt):
                    for h in (0, 1):
                        coef[u, i, h * nt + t] = lookup(table, zones[u] + (2 * t + h))

    wait_load(0, True)
    fill_kappa(0)
    fill_kappa(1)
    pltpu.make_async_copy(patch, patch, load_sem.at[6]).wait()
    for c in range(nc):
        for q in range(4):
            src[c, group(q), :] = lookup(stable, patch[c, pl.ds(q, 8, stride=4), :])
    wait_load(0, False)
    boundary(0, 0)
    wait_load(1, True)
    wait_load(1, False)
    for l in (0, last):
        edge_rows(t0, hs, (0,), l, 31)
        edge_rows(lab, ls, (), l, 31)
    start_load(2)
    greeted = (nt - 1) + (tile > 0).astype(jnp.int32) + (tile < nk - 1).astype(jnp.int32)
    pl.semaphore_wait(barrier, greeted)
    halos(0, 0, "start")
    halos(0, 1, "start")
    send_planes(0, 0)
    fill_kappa(last)
    fill_kappa(last - 1)
    boundary(0, 1)
    send_planes(0, 1)
    for l in (0, last):
        edge_rows(kk, ks, (), l)
    wait_load(2, True)
    wait_load(2, False)

    @pl.loop(1, last)
    def _(l):
        edge_rows(t0, hs, (0,), l, 31)
        edge_rows(lab, ls, (), l, 31)

    halos(0, 2, "start")
    clear_outside()
    pltpu.make_async_copy(zone, zone, load_sem.at[7]).wait()
    fill_coefficients(0, block // 2)
    halos(0, 0, "recv")
    halos(0, 1, "recv")
    send_edges(0)
    halos(0, 3, "start")
    fill_coefficients(block // 2, block)
    solve(0, 1)
    halos(0, 5, "start")

    @pl.loop(2, last - 1)
    def _(l):
        fill_kappa(l)

    solve(0, 0)
    halos(0, 4, "start")
    halos(0, 2, "recv")
    halos(0, 3, "recv")

    @pl.loop(1, cut + 1)
    def _(l):
        inner(0, l)

    halos(1, 2, "start")
    halos(0, 5, "recv")
    inner(0, last - 1)
    halos(0, 4, "recv")

    @pl.loop(cut + 1, cut2 + 1)
    def _(l):
        inner(0, l)

    for h in (0, 1):
        wait_back(0, h, 1)
        wait_back(0, h, 0)
        boundary(1, h)
        send_planes(1, h)
    for h in (0, 1):
        edge_rows(t1, hs, (1,), h * last)

    @pl.loop(cut2 + 1, last - 1)
    def _(l):
        inner(0, l)

    edges_across("recv")
    send_edges(1)
    halos(1, 3, "start")
    halos(1, 2, "recv")

    @pl.loop(2, cut + 1)
    def _(l):
        inner(1, l)

    solve(1, 1)
    inner(1, 1)
    solve(1, 0)
    halos(1, 3, "recv")

    @pl.loop(cut + 1, last)
    def _(l):
        inner(1, l)

    for part, qs in ((1, (1, 2)), (0, (0, 3))):
        for h in (0, 1):
            wait_back(1, h, part)
            for c in range(nc):
                for q in qs:
                    t2[h * last, c, pl.ds(q, 8, stride=4), :] = back[h, c, group(q), :]

    for step in range(STEPS):
        for h, part in chunks:
            for d in order:
                forward(step, h, part, d).wait_send()
                backward(step, h, part, d).wait_send()
        for d in order:
            edge_forward(step, d).wait_send()
    edges_across("send")
    for step, what in ((0, 0), (0, 1), (0, 2), (0, 3), (0, 4), (0, 5), (1, 2), (1, 3)):
        halos(step, what, "send")


def put_kernel(source, out, sem):
    copies = [
        pltpu.make_async_copy(source.at[:, c], out.at[:, :, pl.ds(128 * c, 128)], sem)
        for c in range(source.shape[1])
    ]
    for copy in copies:
        copy.start()
    pltpu.make_async_copy(source, source, sem).wait()


def make_local(mesh):
    nt, nk = mesh.shape["tier"], mesh.shape["tile"]

    def local(temperature, labels, zones, patches, kappa, power, operators):
        _, nl, rows, cols = temperature.shape
        nc = cols // 128
        regions, block, _ = operators.shape
        dims = (nt, nk, nl, nc, regions)
        per = nc // nt

        any_spec = pl.BlockSpec(memory_space=pl.ANY)
        vmem = pl.BlockSpec(memory_space=pltpu.VMEM)
        dma = pltpu.SemaphoreType.DMA
        out = pl.pallas_call(
            functools.partial(heat_kernel, dims),
            out_shape=pltpu.VMEM((nl, nc, 32, 128), F32),
            in_specs=[any_spec] * 7,
            out_specs=vmem,
            scratch_shapes=[
                pltpu.VMEM((nl, nc, 32, 128), F32),
                pltpu.VMEM((nl, nc, 32, 128), jnp.int32),
                pltpu.VMEM((nl, nc, 32, 128), F32),
                pltpu.VMEM((nl, nc, 32, 128), F32),
                pltpu.VMEM((per, 32, 128), jnp.int32),
                pltpu.VMEM((nc, 32, 128), jnp.int32),
                pltpu.VMEM((nc, 32, 128), F32),
                pltpu.VMEM((per * 4, block, block, 8, 128), F32),
                pltpu.VMEM((STEPS, 2, nc, 32, 128), F32),
                pltpu.VMEM((STEPS, 2, nt, per, 32, 128), F32),
                pltpu.VMEM((STEPS, 2, nt, per, 32, 128), F32),
                pltpu.VMEM((STEPS, 2, nl * nc, 128), F32),
                pltpu.VMEM((STEPS, 2, nl * nc, 128), F32),
                pltpu.VMEM((2, nl * nc, 128), F32),
                pltpu.VMEM((2, nl * nc, 128), F32),
                pltpu.VMEM((2, nl * nc, 128), jnp.int32),
                pltpu.VMEM((2, nl * nc, 128), jnp.int32),
                pltpu.VMEM((8, 128), F32),
                pltpu.VMEM((block, 128), F32),
                pltpu.VMEM((2, 2, nc, 128), F32),
                pltpu.VMEM((STEPS, 8 * nt, 128), F32),
                pltpu.VMEM((STEPS, 8 * nt, 128), F32),
                pltpu.VMEM((8 * nt, 128), F32),
                pltpu.VMEM((2, 8 * nt, 128), F32),
                pltpu.VMEM((2, nc, 32, 128), F32),
                pltpu.VMEM((1, kappa.shape[0]), F32),
                pltpu.VMEM((1, power.shape[1]), F32),
                pltpu.VMEM((regions, block, block), F32),
                dma((8,)),
                dma((3,)),
                dma((STEPS, 6, 2)),
                dma((STEPS, 6, 2)),
                dma((6, 2)),
                dma((6, 2)),
                dma((STEPS, 2, 2, nt)),
                dma((STEPS, 2, 2, nt)),
                dma((STEPS, 2, 2, nt)),
                dma((STEPS, 2, 2, nt)),
                dma((3, STEPS, 2, 2)),
                dma((STEPS, nt)),
                dma((STEPS, nt)),
                dma((2, nt)),
                dma((2, nt)),
            ],
            compiler_params=pltpu.CompilerParams(
                collective_id=0, has_side_effects=True, vmem_limit_bytes=62_800_000
            ),
            name="heat",
        )(temperature, labels, zones, patches, kappa[None], power, operators)
        out = pl.pallas_call(
            put_kernel,
            out_shape=jax.ShapeDtypeStruct((nl, rows, cols), F32),
            in_specs=[any_spec],
            out_specs=any_spec,
            scratch_shapes=[dma],
            compiler_params=pltpu.CompilerParams(vmem_limit_bytes=1024 * 1024),
            name="put",
        )(out)
        return out[None]

    return local


def solution(mesh):
    in_specs = (
        P("tier", None, "tile", None),
        P("tier", None, "tile", None),
        P("tile", None),
        P("tier", "tile", None),
        P(),
        P("tier", None),
        P(),
    )
    out_specs = P("tier", None, "tile", None)
    return jax.shard_map(make_local(mesh), mesh=mesh, in_specs=in_specs, out_specs=out_specs, check_vma=False)
```
